512 devices in a mesh: seq: 64 (over x, y, z_lo), head: 8 (over z_hi, core).
Axes of the slice: x: 4, y: 8, z: 8 (z_hi: 4, z_lo: 2; z = z_hi * 2 + z_lo), core: 2. Of those that a mesh axis runs over, the one named last changes fastest.
Arguments:
- queries: bfloat16 [1, 65536, 2048], P(None, 'seq', 'head'), may hold values from -6 to 6
- keys: bfloat16 [1, 65536, 2048], P(None, 'seq', 'head'), may hold values from -6 to 6
- values: bfloat16 [1, 65536, 2048], P(None, 'seq', 'head'), may hold values from -6 to 6
- rates: float32 [1, 16, 65536], P(None, 'head', 'seq'), may hold values from 0.002 to 0.02
- decays: float32 [1, 16, 64], P(None, 'head'), may hold values from 0.02 to 1
- fast_in: bfloat16 [16, 128, 256], P('head'), may hold values from -5 to 5
- fast_out: bfloat16 [16, 128, 128], P('head'), may hold values from -0.5 to 0.5
- ttt_gain: float32 [2048], P('head'), may hold values from 0.25 to 1.75
- out_weight: bfloat16 [2048, 2048], P(None, 'head'), may hold values from -0.125 to 0.125
Outputs:
- layer_out: bfloat16 [1, 65536, 2048], P(None, 'seq', 'head')
The draws below stay inside these ranges and needn't reach their ends.
All inputs are finite; a program needn't handle non-finite values.
Results may differ from the reference program's by a relative error of at most 0.017.
Values may be sent and summed in bfloat16 or wider, within the bound.
A program may use at most 128 MiB of HBM per device.

```python
import math
import jax
import jax.numpy as jnp
from jax import lax

D = 2048
HEADS = 16
DH = 128
FH = 128
BLOCK = 1024
SEQS = 1
UPDATE_BLOCKS = 64
LENGTH = 65536


def draw_pair(key):
    random_seed_key = jax.random.fold_in(key, 7101)
    complete_shape = (SEQS, LENGTH, HEADS * DH)
    query_vals = jnp.clip(1.58 * jax.random.normal(jax.random.fold_in(random_seed_key, 1), complete_shape, jnp.float32), -6.0, 6.0)
    key_vals = jnp.clip(1.58 * jax.random.normal(jax.random.fold_in(random_seed_key, 2), complete_shape, jnp.float32), -6.0, 6.0)
    return (query_vals, key_vals)


def draw_queries(key, part):
    return draw_pair(key)[0].astype(jnp.bfloat16)


def draw_keys(key, part):
    return draw_pair(key)[1].astype(jnp.bfloat16)


def draw_decays(key, part):
    random_seed_key = jax.random.fold_in(key, 5303)
    complete_shape = (SEQS, HEADS, UPDATE_BLOCKS)
    slow_share = 0.5
    slow_mask = jax.random.bernoulli(jax.random.fold_in(random_seed_key, 1), slow_share, (SEQS, HEADS, 1))
    chain_keep = jax.random.uniform(jax.random.fold_in(random_seed_key, 2), (SEQS, HEADS, 1), jnp.float32, 0.4, 0.7)
    jitter = jax.random.uniform(jax.random.fold_in(random_seed_key, 3), complete_shape, jnp.float32, 0.5, 2.0)
    gentle_rate = jnp.exp(jnp.log(chain_keep) * jitter / (1.25 * UPDATE_BLOCKS))
    spike_mask = jax.random.bernoulli(jax.random.fold_in(random_seed_key, 4), 3.0 / UPDATE_BLOCKS, complete_shape)
    spike_keep_flags = jax.random.uniform(jax.random.fold_in(random_seed_key, 5), complete_shape, jnp.float32, 0.6, 0.8)
    gentle_rate = jnp.where(spike_mask, gentle_rate * spike_keep_flags, gentle_rate)
    fast_rate = jnp.exp(jax.random.uniform(jax.random.fold_in(random_seed_key, 6), complete_shape, jnp.float32, jnp.log(0.02), jnp.log(0.2)))
    return jnp.where(slow_mask, gentle_rate, fast_rate).astype(jnp.float32)


def block_scale(rng, extent, pieces, smallest, top_value):
    factor_of, own = 1.0, jax.random.fold_in(rng, 6)
    for position, blocks in pieces:
        steps = jnp.exp(jax.random.uniform(jax.random.fold_in(own, position), (blocks,), jnp.float32, smallest / len(pieces), top_value / len(pieces)))
        factor_of = factor_of * jnp.repeat(steps, extent[position] // blocks).reshape([-1 if axis == position else 1 for axis in range(len(extent))])
    return factor_of


def normal_values(key, extent, scale, bound, shards=(), kind=jnp.bfloat16):
    entries = scale * jax.random.normal(key, extent, jnp.float32)
    if shards:
        entries = entries * block_scale(key, extent, shards, -0.22, 0.18)
    return jnp.clip(entries, -bound, bound).astype(kind)


def setup_inputs(seed: int = 0) -> dict:
    splits = jax.random.split(jax.random.key(seed), 10)
    return {
        "queries": draw_queries(jax.random.fold_in(splits[9], 71), 0),
        "keys": draw_keys(jax.random.fold_in(splits[9], 71), 0),
        "values": normal_values(splits[2], (SEQS, LENGTH, HEADS * DH), 1.0, 6.0, ((1, 64), (2, 8))),
        "rates": jnp.clip(jnp.exp(math.log(0.02) - 2.30258502 * jax.random.uniform(splits[3], (SEQS, HEADS, LENGTH), jnp.float32) ** block_scale(splits[3], (SEQS, HEADS, LENGTH), ((1, 8), (2, 64)), -0.2, 0.2)), 0.002, 0.02),
        "decays": draw_decays(jax.random.fold_in(splits[9], 71), 0),
        "fast_in": normal_values(splits[5], (HEADS, DH, 2 * FH), 1.0, 5.0, ((0, 8),)),
        "fast_out": normal_values(splits[6], (HEADS, FH, DH), FH ** -0.5, 0.5, ((0, 8),)),
        "ttt_gain": jnp.clip(1.0 + 0.15 * jax.random.normal(splits[7], (HEADS * DH,), jnp.float32), 0.25, 1.75),
        "out_weight": normal_values(splits[8], (HEADS * DH, D), (HEADS * DH) ** -0.5, 0.125, ((1, 8),)),
    }


EPSILON = 1e-06

def unit_rows(matrix):
    widened = matrix.astype(jnp.float32)
    guarded = lax.optimization_barrier(jnp.sum(widened * widened, axis=-1, keepdims=True)) + EPSILON
    return (widened * lax.rsqrt(guarded)).astype(jnp.bfloat16)

def swish_product(raw_rows):
    half_width = raw_rows.shape[-1] // 2
    gate_part = raw_rows[..., :half_width]
    return gate_part * jax.nn.sigmoid(gate_part) * raw_rows[..., half_width:]

def block_deltas(key_unit, value_rows, rate_rows, weight_in, weight_out):
    raw_gate = jnp.dot(key_unit, weight_in, preferred_element_type=jnp.float32)
    half_width = raw_gate.shape[-1] // 2
    gate_part = raw_gate[:, :half_width]
    up_part = raw_gate[:, half_width:]
    gate_sigmoid = jax.nn.sigmoid(gate_part)
    hidden_keys = (gate_part * gate_sigmoid * up_part).astype(jnp.bfloat16)
    signal = (rate_rows[:, None] * value_rows.astype(jnp.float32)).astype(jnp.bfloat16)
    delta_out = jnp.dot(hidden_keys.T, signal, preferred_element_type=jnp.float32)
    back_signal = jnp.dot(signal, weight_out.T, preferred_element_type=jnp.float32)
    grad_in = jnp.concatenate([back_signal * up_part * gate_sigmoid * (1.0 + gate_part * (1.0 - gate_sigmoid)), back_signal * gate_part * gate_sigmoid], axis=-1).astype(jnp.bfloat16)
    delta_in = jnp.dot(key_unit.T, grad_in, preferred_element_type=jnp.float32)
    return (delta_in, delta_out)

def recall(query_unit, state_in, state_out):
    raw_query = jnp.dot(query_unit, state_in.astype(jnp.bfloat16), preferred_element_type=jnp.float32)
    hidden_queries = swish_product(raw_query).astype(jnp.bfloat16)
    return jnp.dot(hidden_queries, state_out.astype(jnp.bfloat16), preferred_element_type=jnp.float32)

def window_rows(query_rows, key_span, value_span, block_index):
    block_len = query_rows.shape[0]
    query_block = min(512, block_len)
    score_scale = query_rows.shape[-1] ** (-0.5)
    segment_parts = []
    for row_start in range(0, block_len, query_block):
        query_part = query_rows[row_start:row_start + query_block]
        key_part = key_span[row_start:row_start + 2 * block_len + query_block]
        value_part = value_span[row_start:row_start + 2 * block_len + query_block]
        scores = jnp.dot(query_part, key_part.T, preferred_element_type=jnp.float32) * score_scale
        query_pos = block_index * block_len + row_start + lax.broadcasted_iota(jnp.int32, scores.shape, 0)
        key_pos = (block_index - 2) * block_len + row_start + lax.broadcasted_iota(jnp.int32, scores.shape, 1)
        in_window = (key_pos <= query_pos) & (key_pos > query_pos - 2 * block_len) & (key_pos >= 0)
        masked = jnp.where(in_window, scores, -jnp.inf)
        highest = lax.optimization_barrier(jnp.max(masked, axis=-1, keepdims=True))
        exp_scores = jnp.exp(masked - highest)
        weights = (exp_scores / lax.optimization_barrier(jnp.sum(exp_scores, axis=-1, keepdims=True))).astype(jnp.bfloat16)
        segment_parts.append(jnp.dot(weights, value_part, preferred_element_type=jnp.float32))
    return jnp.concatenate(segment_parts, axis=0)

def one_sequence(query_rows, key_rows, value_rows, rate_rows, decay_rows, weight_in, weight_out, gain_rows):
    query_unit = unit_rows(query_rows)
    key_unit = unit_rows(key_rows)
    zero_rows = jnp.zeros((2 * BLOCK, DH), jnp.bfloat16)
    padded_keys = jnp.concatenate([zero_rows, key_rows], axis=0)
    padded_values = jnp.concatenate([zero_rows, value_rows], axis=0)

    def attend(block_index):
        first_row = block_index * BLOCK
        key_span = lax.dynamic_slice_in_dim(padded_keys, first_row, 3 * BLOCK, 0)
        value_span = lax.dynamic_slice_in_dim(padded_values, first_row, 3 * BLOCK, 0)
        query_here = lax.dynamic_slice_in_dim(query_rows, first_row, BLOCK, 0)
        return window_rows(query_here, key_span, value_span, block_index)
    attended = lax.map(attend, jnp.arange(UPDATE_BLOCKS, dtype=jnp.int32))

    def advance(carry, inputs):
        state_in, state_out = carry
        key_block, value_block, rate_block, query_block, decay_now = inputs
        recalled = recall(query_block, state_in, state_out)
        delta_in, delta_out = block_deltas(key_block, value_block, rate_block, weight_in, weight_out)
        return ((decay_now * state_in + delta_in, decay_now * state_out + delta_out), recalled)
    start_state = (weight_in.astype(jnp.float32), weight_out.astype(jnp.float32))
    inputs = (key_unit.reshape(UPDATE_BLOCKS, BLOCK, DH), value_rows.reshape(UPDATE_BLOCKS, BLOCK, DH), rate_rows.reshape(UPDATE_BLOCKS, BLOCK), query_unit.reshape(UPDATE_BLOCKS, BLOCK, DH), decay_rows)
    final_state, recalled = lax.scan(advance, start_state, inputs)
    mean_square = lax.optimization_barrier(jnp.mean(recalled * recalled, axis=-1, keepdims=True)) + EPSILON
    normed = recalled * lax.rsqrt(mean_square) * gain_rows
    return (attended + normed).astype(jnp.bfloat16).reshape(LENGTH, DH)

def reference(queries, keys, values, rates, decays, fast_in, fast_out, ttt_gain, out_weight):

    def per_head(head_index):
        column = head_index * DH
        query_all = lax.dynamic_slice_in_dim(queries, column, DH, 2)
        key_all = lax.dynamic_slice_in_dim(keys, column, DH, 2)
        value_all = lax.dynamic_slice_in_dim(values, column, DH, 2)
        rate_all = lax.dynamic_index_in_dim(rates, head_index, 1, keepdims=False)
        decay_all = lax.dynamic_index_in_dim(decays, head_index, 1, keepdims=False)
        weight_in = lax.dynamic_index_in_dim(fast_in, head_index, 0, keepdims=False)
        weight_out = lax.dynamic_index_in_dim(fast_out, head_index, 0, keepdims=False)
        gain_rows = lax.dynamic_slice_in_dim(ttt_gain, column, DH, 0)
        results = [one_sequence(query_all[seq_index], key_all[seq_index], value_all[seq_index], rate_all[seq_index], decay_all[seq_index], weight_in, weight_out, gain_rows) for seq_index in range(SEQS)]
        return jnp.stack(results)
    mixed_heads = lax.map(per_head, jnp.arange(HEADS, dtype=jnp.int32))
    combined = jnp.transpose(mixed_heads, (1, 2, 0, 3)).reshape(SEQS * LENGTH, HEADS * DH)
    projected = jnp.dot(combined, out_weight, preferred_element_type=jnp.float32)
    return projected.reshape(SEQS, LENGTH, D).astype(jnp.bfloat16)
```

```python
import functools

import jax
import jax.numpy as jnp
from jax import lax
from jax.experimental import pallas as pl
from jax.experimental.pallas import tpu as pltpu
from jax.sharding import PartitionSpec as P

EPSILON = 1e-06
MESH = pl.DeviceIdType.MESH
F32 = jnp.float32
BF16 = jnp.bfloat16

PAIR = 2
COLUMN = 16
COLUMNS = 4
HEAD_DEVICES = 8
LOG2E = 1.4426950408889634

KV_CHUNKS = 8
GATHER_CHUNKS = 8
QUERY_ROWS = 256


def remote(src, dst, send_sem, recv_sem, device_id):
    return pltpu.make_async_remote_copy(
        src_ref=src,
        dst_ref=dst,
        send_sem=send_sem,
        recv_sem=recv_sem,
        device_id=device_id,
        device_id_type=MESH,
    )


def layer_kernel(
    q_ref, k_hbm, v_hbm, rates_ref, decays_ref, fin_ref, fout_ref, gain_ref, w_ref, o_ref,
    kv, rate_cols, dacc, dsend, drecv, tsend, trecv, ssend, states, gath,
    load_sem, far_send, far_recv, near_send, near_recv, d_send, d_recv,
    t_send, t_recv, s_send, s_recv, g_send, g_recv,
):
    place = lax.axis_index("seq")
    head_place = lax.axis_index("head")
    blocks = COLUMN * COLUMNS
    block_len = q_ref.shape[0]
    heads_here, dh = fin_ref.shape[0], fin_ref.shape[1]
    z_lo = lax.rem(place, PAIR)
    column = lax.div(place, COLUMN)
    rung = lax.rem(place, COLUMN)
    partner_block = place + 1 - 2 * z_lo
    two_on = lax.rem(place + 2, blocks)
    two_back = lax.rem(place + blocks - 2, blocks)
    z_hi = lax.div(head_place, 2)
    core = lax.rem(head_place, 2)
    right = lax.rem(z_hi + 1, 4) * 2 + core
    left = lax.rem(z_hi + 3, 4) * 2 + core
    across = lax.rem(z_hi + 2, 4) * 2 + core
    twin = z_hi * 2 + 1 - core

    def column_peer(step):
        return column * COLUMN + lax.rem(rung + step, COLUMN)

    def row_peer(step):
        return lax.rem(column + step, COLUMNS) * COLUMN + rung

    own_base = 2 * block_len
    loads = [
        pltpu.make_async_copy(k_hbm, kv.at[0, pl.ds(own_base, block_len)], load_sem.at[0]),
        pltpu.make_async_copy(v_hbm, kv.at[1, pl.ds(own_base, block_len)], load_sem.at[1]),
    ]
    for load in loads:
        load.start()
    barrier = pltpu.get_barrier_semaphore()
    for peer in (two_on, two_back):
        pl.semaphore_signal(barrier, inc=1, device_id={"seq": peer}, device_id_type=MESH)
    for peer in (left, right, twin):
        pl.semaphore_signal(barrier, inc=1, device_id={"head": peer}, device_id_type=MESH)

    def greet_column(step, _):
        pl.semaphore_signal(barrier, inc=1, device_id={"seq": column_peer(step)}, device_id_type=MESH)
        return 0

    def greet_row(step, _):
        pl.semaphore_signal(barrier, inc=1, device_id={"seq": row_peer(step)}, device_id_type=MESH)
        return 0

    lax.fori_loop(1, COLUMN, greet_column, 0)
    lax.fori_loop(1, COLUMNS, greet_row, 0)
    for load in loads:
        load.wait()
    pl.semaphore_wait(barrier, 2 + 3 + (COLUMN - 1) + (COLUMNS - 1))

    kv_rows = block_len // KV_CHUNKS

    def far_copy(c):
        rows = pl.multiple_of(c * kv_rows, kv_rows)
        return remote(
            kv.at[:, pl.ds(own_base + rows, kv_rows)],
            kv.at[:, pl.ds(rows, kv_rows)],
            far_send.at[c], far_recv.at[c], {"seq": two_on},
        )

    def near_copy(c, source_base):
        rows = pl.multiple_of(c * kv_rows, kv_rows)
        return remote(
            kv.at[:, pl.ds(source_base + rows, kv_rows)],
            kv.at[:, pl.ds(block_len + rows, kv_rows)],
            near_send.at[c], near_recv.at[c], {"seq": partner_block},
        )

    def send_kv(c, _):
        far_copy(c).start()

        @pl.when(z_lo == 0)
        def _():
            near_copy(c, own_base).start()

        return 0

    lax.fori_loop(0, KV_CHUNKS, send_kv, 0)

    def relay_kv(c, _):
        far_copy(c).wait_recv()

        @pl.when(z_lo == 1)
        def _():
            near_copy(c, 0).start()

        return 0

    rates8 = jnp.concatenate([rates_ref[...]] * 4, axis=0)
    rate_cols[...] = jnp.transpose(rates8)
    for h in range(heads_here):
        columns = slice(h * dh, (h + 1) * dh)
        w_in = fin_ref[h]
        w_out = fout_ref[h]
        for r in range(0, block_len, QUERY_ROWS):
            keys = kv[0, own_base + r : own_base + r + QUERY_ROWS, columns].astype(F32)
            values = kv[1, own_base + r : own_base + r + QUERY_ROWS, columns].astype(F32)
            norm = lax.rsqrt(jnp.sum(keys * keys, axis=-1, keepdims=True) + EPSILON)
            key_unit = (keys * norm).astype(BF16)
            raw = jnp.dot(key_unit, w_in, preferred_element_type=F32)
            gate, up = raw[:, :dh], raw[:, dh:]
            sig = jax.nn.sigmoid(gate)
            hidden = (gate * sig * up).astype(BF16)
            signal = (rate_cols[r : r + QUERY_ROWS, h : h + 1] * values).astype(BF16)
            back = lax.dot_general(signal, w_out, (((1,), (1,)), ((), ())), preferred_element_type=F32)
            grad = jnp.concatenate(
                [
                    (back * up * sig * (1.0 + gate * (1.0 - sig))).astype(BF16),
                    (back * gate * sig).astype(BF16),
                ],
                axis=-1,
            )
            d_in = lax.dot_general(key_unit, grad, (((0,), (0,)), ((), ())), preferred_element_type=F32)
            d_out = lax.dot_general(hidden, signal, (((0,), (0,)), ((), ())), preferred_element_type=F32)
            if r == 0:
                dacc[h, :, : 2 * dh] = d_in
                dacc[h, :, 2 * dh :] = d_out
            else:
                dacc[h, :, : 2 * dh] += d_in
                dacc[h, :, 2 * dh :] += d_out
    slices = dsend.shape[0]
    dsend[...] = dacc[...].reshape(dsend.shape).astype(BF16)

    def d_copy(step):
        target = lax.rem(rung + step, COLUMN)
        return remote(
            dsend.at[target], drecv.at[rung], d_send.at[step], d_recv.at[step],
            {"seq": column_peer(step)},
        )

    def d_wait(step, _):
        source = lax.rem(rung + COLUMN - step, COLUMN)
        remote(
            dsend.at[source], drecv.at[source], d_send.at[step], d_recv.at[step],
            {"seq": column_peer(step)},
        ).wait_recv()
        return 0

    def start(make):
        def one(step, _):
            make(step).start()
            return 0
        return one

    def drain(make):
        def one(step, _):
            make(step).wait_send()
            return 0
        return one

    lax.fori_loop(1, COLUMN, start(d_copy), 0)
    drecv[rung] = dsend[rung]

    lax.fori_loop(0, 4, relay_kv, 0)
    lax.fori_loop(1, COLUMN, d_wait, 0)

    slice_head = lax.div(rung, COLUMN // heads_here)

    def decay_at(index):
        return decays_ref[slice_head, index]

    def fold_in(i, total):
        return decay_at(column * COLUMN + i) * total + drecv[i].astype(F32)

    tsend[...] = lax.fori_loop(0, COLUMN, fold_in, jnp.zeros(tsend.shape, F32))

    def t_copy(step):
        return remote(
            tsend, trecv.at[column], t_send.at[step], t_recv.at[step], {"seq": row_peer(step)}
        )

    def t_wait(step, _):
        source = lax.rem(column + COLUMNS - step, COLUMNS)
        remote(
            tsend, trecv.at[source], t_send.at[step], t_recv.at[step], {"seq": row_peer(step)}
        ).wait_recv()
        return 0

    lax.fori_loop(1, COLUMNS, start(t_copy), 0)
    trecv[column] = tsend[...]
    lax.fori_loop(4, 6, relay_kv, 0)
    lax.fori_loop(1, COLUMNS, t_wait, 0)

    slice_row = lax.rem(rung, COLUMN // heads_here) * (dh * heads_here // COLUMN)
    slice_rows = pl.ds(pl.multiple_of(slice_row, 16), tsend.shape[0])
    state = jnp.concatenate(
        [fin_ref[slice_head, slice_rows].astype(F32), fout_ref[slice_head, slice_rows].astype(F32)], axis=-1
    )
    for c in range(COLUMNS - 1):
        kept = lax.fori_loop(0, COLUMN, lambda i, f: f * decay_at(c * COLUMN + i), jnp.float32(1.0))
        passed = c < column
        state = jnp.where(passed, kept, 1.0) * state + jnp.where(passed, 1.0, 0.0) * trecv[c]

    def advance(i, state):
        ssend[i] = state.astype(BF16)
        return decay_at(column * COLUMN + i) * state + drecv[i].astype(F32)

    lax.fori_loop(0, COLUMN, advance, state)

    def s_copy(step):
        target = lax.rem(rung + step, COLUMN)
        return remote(
            ssend.at[target], states.at[rung], s_send.at[step], s_recv.at[step],
            {"seq": column_peer(step)},
        )

    def s_wait(step, _):
        source = lax.rem(rung + COLUMN - step, COLUMN)
        remote(
            ssend.at[source], states.at[source], s_send.at[step], s_recv.at[step],
            {"seq": column_peer(step)},
        ).wait_recv()
        return 0

    lax.fori_loop(1, COLUMN, start(s_copy), 0)
    states[rung] = ssend[rung]
    lax.fori_loop(6, KV_CHUNKS, relay_kv, 0)

    def near_wait(c, _):
        near_copy(c, 0).wait_recv()
        return 0

    lax.fori_loop(1, COLUMN, s_wait, 0)
    lax.fori_loop(0, KV_CHUNKS, near_wait, 0)

    gather_rows = block_len // GATHER_CHUNKS
    pieces = QUERY_ROWS // gather_rows

    def gather_copy(kind, source, target, c):
        rows = pl.ds(pl.multiple_of(c * gather_rows, gather_rows), gather_rows)
        return remote(
            gath.at[source, rows], gath.at[source, rows],
            g_send.at[kind, c], g_recv.at[kind, c], {"head": target},
        )

    span = 2 * block_len + QUERY_ROWS
    first_valid = (2 - jnp.minimum(place, 2)) * block_len
    scale = LOG2E * dh ** (-0.5)

    def rows_of(rc, _):
        row0 = pl.multiple_of(rc * QUERY_ROWS, QUERY_ROWS)
        local_valid = first_valid - row0
        row_ids = lax.broadcasted_iota(jnp.int32, (QUERY_ROWS, QUERY_ROWS), 0)
        col_ids = lax.broadcasted_iota(jnp.int32, (QUERY_ROWS, QUERY_ROWS), 1)
        middle_ids = lax.broadcasted_iota(jnp.int32, (1, span - 2 * QUERY_ROWS), 1) + QUERY_ROWS
        middle_bias = jnp.where(middle_ids >= local_valid, 0.0, -1e30).astype(F32)
        for h in range(heads_here):
            columns = slice(h * dh, (h + 1) * dh)
            queries = q_ref[pl.ds(row0, QUERY_ROWS), columns]
            keys = kv[0, pl.ds(row0, span), columns]
            scores = lax.dot_general(queries, keys, (((1,), (1,)), ((), ())), preferred_element_type=F32)
            head_part = jnp.where(
                (col_ids > row_ids) & (col_ids >= local_valid), scores[:, :QUERY_ROWS], -1e30
            )
            middle_part = scores[:, QUERY_ROWS : span - QUERY_ROWS] + middle_bias
            tail_part = jnp.where(col_ids <= row_ids, scores[:, span - QUERY_ROWS :], -1e30)
            scores = jnp.concatenate([head_part, middle_part, tail_part], axis=-1)
            highest = jnp.max(scores, axis=-1, keepdims=True)
            weights = jnp.exp2((scores - highest) * scale).astype(BF16)
            values = kv[1, pl.ds(row0, span), columns]
            widened = jnp.concatenate([values, jnp.ones_like(values)], axis=-1)
            summed = jnp.dot(weights, widened, preferred_element_type=F32)
            attended = summed[:, :dh] / summed[:, dh:]

            q_wide = queries.astype(F32)
            q_norm = lax.rsqrt(jnp.sum(q_wide * q_wide, axis=-1, keepdims=True) + EPSILON)
            q_unit = (q_wide * q_norm).astype(BF16)
            per_head = COLUMN // heads_here
            state_h = states[h * per_head : (h + 1) * per_head].reshape(dh, 3 * dh)
            raw = jnp.dot(q_unit, state_h[:, : 2 * dh], preferred_element_type=F32)
            gate = raw[:, :dh]
            hidden = (gate * jax.nn.sigmoid(gate) * raw[:, dh:]).astype(BF16)
            recalled = jnp.dot(hidden, state_h[:, 2 * dh :], preferred_element_type=F32)
            mean_square = jnp.mean(recalled * recalled, axis=-1, keepdims=True) + EPSILON
            normed = recalled * lax.rsqrt(mean_square) * gain_ref[:, columns]
            gath[head_place, pl.ds(row0, QUERY_ROWS), columns] = (attended + normed).astype(BF16)
        for piece in range(pieces):
            c = rc * pieces + piece
            gather_copy(0, head_place, right, c).start()
            gather_copy(1, head_place, left, c).start()
            gather_copy(3, head_place, twin, c).start()
        return 0

    lax.fori_loop(0, block_len // QUERY_ROWS, rows_of, 0)

    left_twin = lax.rem(z_hi + 3, 4) * 2 + 1 - core
    right_twin = lax.rem(z_hi + 1, 4) * 2 + 1 - core
    across_twin = lax.rem(z_hi + 2, 4) * 2 + 1 - core

    def relay(c2, _):
        for odd in range(2):
            c = 2 * c2 + odd
            gather_copy(0, left, right, c).wait_recv()
            if odd == 0:
                gather_copy(2, left, right, c).start()
            gather_copy(4, left, twin, c).start()
            gather_copy(1, right, left, c).wait_recv()
            if odd == 1:
                gather_copy(2, right, left, c).start()
            gather_copy(5, right, twin, c).start()
        return 0

    lax.fori_loop(0, GATHER_CHUNKS // 2, relay, 0)

    def last_hop(c, _):
        gather_copy(2, across, left, c).wait_recv()
        gather_copy(6, across, twin, c).start()
        return 0

    lax.fori_loop(0, GATHER_CHUNKS, last_hop, 0)

    def project(c, _):
        gather_copy(3, twin, twin, c).wait_recv()
        gather_copy(4, left_twin, twin, c).wait_recv()
        gather_copy(5, right_twin, twin, c).wait_recv()
        gather_copy(6, across_twin, twin, c).wait_recv()
        rows = pl.ds(pl.multiple_of(c * gather_rows, gather_rows), gather_rows)
        width = gath.shape[2]
        total = jnp.zeros((gather_rows, width), F32)
        for h in range(HEAD_DEVICES):
            total += jnp.dot(
                gath[h, rows, :], w_ref[h * width : (h + 1) * width, :], preferred_element_type=F32
            )
        o_ref[rows, :] = total.astype(BF16)
        return 0

    lax.fori_loop(0, GATHER_CHUNKS, project, 0)

    def drain_kv(c, _):
        far_copy(c).wait_send()
        near_copy(c, 0).wait_send()
        return 0

    def drain_gather(c, _):
        for kind in range(7):
            gather_copy(kind, head_place, twin, c).wait_send()
        return 0

    lax.fori_loop(0, KV_CHUNKS, drain_kv, 0)
    lax.fori_loop(1, COLUMN, drain(d_copy), 0)
    lax.fori_loop(1, COLUMNS, drain(t_copy), 0)
    lax.fori_loop(1, COLUMN, drain(s_copy), 0)
    lax.fori_loop(0, GATHER_CHUNKS, drain_gather, 0)


def local(queries, keys, values, rates, decays, fast_in, fast_out, ttt_gain, out_weight):
    seq_count, block_len, width = queries.shape
    heads_here, dh, _ = fast_in.shape
    rows = heads_here * dh // COLUMN
    vmem = pl.BlockSpec(memory_space=pltpu.VMEM)
    smem = pl.BlockSpec(memory_space=pltpu.SMEM)
    anywhere = pl.BlockSpec(memory_space=pl.ANY)
    dma = pltpu.SemaphoreType.DMA
    out = pl.pallas_call(
        layer_kernel,
        out_shape=jax.ShapeDtypeStruct((block_len, width), BF16),
        in_specs=[vmem, anywhere, anywhere, vmem, smem, vmem, vmem, vmem, vmem],
        out_specs=vmem,
        scratch_shapes=[
            pltpu.VMEM((2, 3 * block_len, width), BF16),
            pltpu.VMEM((block_len, 8), F32),
            pltpu.VMEM((heads_here, dh, 3 * dh), F32),
            pltpu.VMEM((COLUMN, rows, 3 * dh), BF16),
            pltpu.VMEM((COLUMN, rows, 3 * dh), BF16),
            pltpu.VMEM((rows, 3 * dh), F32),
            pltpu.VMEM((COLUMNS, rows, 3 * dh), F32),
            pltpu.VMEM((COLUMN, rows, 3 * dh), BF16),
            pltpu.VMEM((COLUMN, rows, 3 * dh), BF16),
            pltpu.VMEM((HEAD_DEVICES, block_len, width), BF16),
            dma((2,)),
            dma((KV_CHUNKS,)), dma((KV_CHUNKS,)), dma((KV_CHUNKS,)), dma((KV_CHUNKS,)),
            dma((COLUMN,)), dma((COLUMN,)),
            dma((COLUMNS,)), dma((COLUMNS,)),
            dma((COLUMN,)), dma((COLUMN,)),
            dma((7, GATHER_CHUNKS)), dma((7, GATHER_CHUNKS)),
        ],
        compiler_params=pltpu.CompilerParams(
            collective_id=0, has_side_effects=True, vmem_limit_bytes=48 << 20
        ),
        name="layer",
    )(
        queries.reshape(block_len, width), keys.reshape(block_len, width), values.reshape(block_len, width),
        rates.reshape(heads_here, block_len), decays.reshape(heads_here, -1),
        fast_in, fast_out, ttt_gain.reshape(1, width), out_weight,
    )
    return out.reshape(seq_count, block_len, width)


def solution(mesh):
    placed = (
        P(None, "seq", "head"),
        P(None, "seq", "head"),
        P(None, "seq", "head"),
        P(None, "head", "seq"),
        P(None, "head", None),
        P("head", None, None),
        P("head", None, None),
        P("head"),
        P(None, "head"),
    )
    return jax.shard_map(
        local, mesh=mesh, in_specs=placed, out_specs=P(None, "seq", "head"), check_vma=False
    )
```

```python
import jax
import jax.numpy as jnp
from jax import lax
from jax.experimental import pallas as pl
from jax.experimental.pallas import tpu as pltpu
from jax.sharding import PartitionSpec as P

EPSILON = 1e-06
MESH = pl.DeviceIdType.MESH
F32 = jnp.float32
BF16 = jnp.bfloat16

COLUMN = 8
COLUMNS = 4
HEADS = 16
ROWS = 256
LOG2E = 1.4426950408889634


def remote(src, dst, send_sem, recv_sem, device_id):
    return pltpu.make_async_remote_copy(
        src_ref=src,
        dst_ref=dst,
        send_sem=send_sem,
        recv_sem=recv_sem,
        device_id=device_id,
        device_id_type=MESH,
    )


def dot(a, b):
    return jnp.dot(a, b, preferred_element_type=F32)


def dot_nt(a, b):
    return lax.dot_general(a, b, (((1,), (1,)), ((), ())), preferred_element_type=F32)


def dot_tn(a, b):
    return lax.dot_general(a, b, (((0,), (0,)), ((), ())), preferred_element_type=F32)


def layer_kernel(
    q_hbm, k_hbm, v_hbm, rates_hbm, decays_ref, fin_hbm, fout_hbm, gain_hbm, w_hbm, o_ref,
    kv, qh, spare, rates_ref, rate_cols, fin_ref, fout_ref, gain_ref, w_ref,
    dsend, dpair, tsend, trecv, usend, urecv, ssend, srecv, states, comb, gath,
    load_sem, pair_sem, q_send, q_recv, e_send, e_recv, far_send, far_recv, t_send, t_recv,
    u_send, u_recv, s_send, s_recv, g_send, g_recv,
):
    place = lax.axis_index("seq")
    head_place = lax.axis_index("head")
    blocks = 2 * COLUMN * COLUMNS
    block_len = q_hbm.shape[0]
    dh = fin_ref.shape[1]
    pieces = block_len // ROWS
    z_lo = lax.rem(place, 2)
    pair = lax.div(place, 2)
    rung = lax.rem(pair, COLUMN)
    column = lax.div(pair, COLUMN)
    z_hi = lax.div(head_place, 2)
    core = lax.rem(head_place, 2)
    partner = place + 1 - 2 * z_lo
    two_on = lax.rem(place + 2, blocks)
    two_back = lax.rem(place + blocks - 2, blocks)

    def at(hops, which):
        return lax.rem(z_hi + hops + 8, 4) * 2 + which

    def head_of(hops, which, low):
        return lax.rem(z_hi + hops + 8, 4) * 4 + which * 2 + low

    up2 = {"head": at(1, core)}
    down2 = {"head": at(-1, core)}
    twin = {"head": at(0, 1 - core)}
    up1 = {"seq": partner, "head": at(z_lo, core)}
    down1 = {"seq": partner, "head": at(z_lo - 1, core)}

    def column_peer(step):
        return {"seq": (column * COLUMN + lax.rem(rung + step, COLUMN)) * 2 + z_lo}

    def row_peer(step):
        return {"seq": (lax.rem(column + step, COLUMNS) * COLUMN + rung) * 2 + z_lo}

    mine = pl.ds(pl.multiple_of(z_lo * dh, dh), dh)
    other = pl.ds(pl.multiple_of((1 - z_lo) * dh, dh), dh)
    own_row = pl.multiple_of(z_lo * block_len, block_len)
    own_base = pl.multiple_of(2 * block_len + z_lo * block_len, block_len)
    own_rows = pl.ds(own_base, block_len)
    load_list = [
        (k_hbm.at[:, mine], kv.at[0, own_rows]),
        (v_hbm.at[:, mine], kv.at[1, own_rows]),
        (k_hbm.at[:, other], spare.at[0]),
        (v_hbm.at[:, other], spare.at[1]),
        (rates_hbm, rates_ref),
        (fin_hbm, fin_ref),
        (fout_hbm, fout_ref),
        (q_hbm.at[:, other], spare.at[2]),
        (q_hbm.at[:, mine], qh.at[pl.ds(own_row, block_len)]),
        (gain_hbm, gain_ref),
        (w_hbm, w_ref),
    ]
    loads = [
        pltpu.make_async_copy(src, dst, load_sem.at[i]) for i, (src, dst) in enumerate(load_list)
    ]
    for load in loads:
        load.start()

    barrier = pltpu.get_barrier_semaphore()

    def greet(device_id):
        pl.semaphore_signal(barrier, inc=1, device_id=device_id, device_id_type=MESH)

    def greet_column(step, _):
        greet(column_peer(step))
        return 0

    def greet_row(step, _):
        greet(row_peer(step))
        return 0

    lax.fori_loop(1, COLUMN, greet_column, 0)
    lax.fori_loop(1, COLUMNS, greet_row, 0)
    for device_id in ({"seq": two_on}, {"seq": two_back}, up1, down1, up2, down2, twin):
        greet(device_id)
    for load in loads[:7]:
        load.wait()

    lower = z_lo == 0
    rates_mine = jnp.where(lower, rates_ref[0:1, :], rates_ref[1:2, :])
    rates_other = jnp.where(lower, rates_ref[1:2, :], rates_ref[0:1, :])
    rate_cols[...] = jnp.transpose(jnp.concatenate([rates_mine, rates_other] * 4, axis=0))
    for which in (1, 0):
        w_in = fin_ref[1 - z_lo] if which else fin_ref[z_lo]
        w_out = fout_ref[1 - z_lo] if which else fout_ref[z_lo]
        d_in = d_out = None
        for r in range(0, block_len, ROWS):
            if which:
                keys, values = spare[0, r : r + ROWS], spare[1, r : r + ROWS]
            else:
                rows = pl.ds(pl.multiple_of(own_base + r, ROWS), ROWS)
                keys, values = kv[0, rows], kv[1, rows]
            keys, values = keys.astype(F32), values.astype(F32)
            norm = lax.rsqrt(jnp.sum(keys * keys, axis=-1, keepdims=True) + EPSILON)
            key_unit = (keys * norm).astype(BF16)
            raw = dot(key_unit, w_in)
            gate, up = raw[:, :dh], raw[:, dh:]
            sig = jax.nn.sigmoid(gate)
            hidden = (gate * sig * up).astype(BF16)
            signal = (rate_cols[r : r + ROWS, which : which + 1] * values).astype(BF16)
            back = dot_nt(signal, w_out)
            grad = jnp.concatenate(
                [
                    (back * up * sig * (1.0 + gate * (1.0 - sig))).astype(BF16),
                    (back * gate * sig).astype(BF16),
                ],
                axis=-1,
            )
            part_in, part_out = dot_tn(key_unit, grad), dot_tn(hidden, signal)
            d_in = part_in if d_in is None else d_in + part_in
            d_out = part_out if d_out is None else d_out + part_out
        delta = jnp.concatenate([d_in, d_out], axis=-1).astype(BF16)
        if which:
            dsend[...] = delta
        else:
            dpair[z_lo] = delta

    pl.semaphore_wait(barrier, (COLUMN - 1) + (COLUMNS - 1) + 7)

    pair_device = {"seq": partner}

    def start(make):
        def one(step, _):
            make(step).start()
            return 0
        return one

    def wait_sent(make):
        def one(step, _):
            make(step).wait_send()
            return 0
        return one

    def wait_got(make):
        def one(step, _):
            make(step).wait_recv()
            return 0
        return one

    d_copy = remote(dsend, dpair.at[z_lo], pair_sem.at[0], pair_sem.at[1], pair_device)

    def q_copy(i):
        row = pl.multiple_of(i * ROWS, ROWS)
        return remote(
            spare.at[2, pl.ds(row, ROWS)],
            qh.at[pl.ds(pl.multiple_of(own_row + row, ROWS), ROWS)],
            q_send.at[i], q_recv.at[i], pair_device,
        )

    def e_copy(i):
        row = pl.multiple_of(i * ROWS, ROWS)
        return remote(
            spare.at[pl.ds(0, 2), pl.ds(row, ROWS)],
            kv.at[:, pl.ds(pl.multiple_of(own_base + row, ROWS), ROWS)],
            e_send.at[i], e_recv.at[i], pair_device,
        )

    def far_copy(c):
        row = pl.multiple_of(c * ROWS, ROWS)
        return remote(
            kv.at[:, pl.ds(pl.multiple_of(2 * block_len + row, ROWS), ROWS)],
            kv.at[:, pl.ds(row, ROWS)],
            far_send.at[c], far_recv.at[c], {"seq": two_on},
        )

    def relay_far(i):
        e_copy(i).wait_recv()
        far_copy((1 - z_lo) * pieces + i).start()

    d_copy.start()

    far_copy((1 + z_lo) * pieces - 1).start()

    loads[7].wait()
    for i in reversed(range(pieces)):
        e_copy(i).start()
    for i in reversed(range(pieces)):
        q_copy(i).start()

    def decay_at(block):
        return decays_ref[z_lo, block]

    def pair_decay(c, r):
        first = (c * COLUMN + r) * 2
        return decay_at(first) * decay_at(first + 1)

    d_copy.wait_recv()
    pair_sum = decay_at(2 * pair + 1) * dpair[0].astype(F32) + dpair[1].astype(F32)
    tsend[...] = pair_sum.astype(BF16).reshape(tsend.shape)

    def t_copy(step):
        target = lax.rem(rung + step, COLUMN)
        return remote(
            tsend.at[target], trecv.at[rung], t_send.at[step], t_recv.at[step], column_peer(step)
        )

    lax.fori_loop(1, COLUMN, start(t_copy), 0)
    trecv[rung] = tsend[rung]

    @pl.when(z_lo == 1)
    def _():
        far_copy(2 * pieces - 2).start()
        far_copy(2 * pieces - 3).start()

    @pl.when(z_lo == 0)
    def _():
        relay_far(3)

    lax.fori_loop(1, COLUMN, wait_got(t_copy), 0)

    def fold_in(r, total):
        return pair_decay(column, r) * total + trecv[r].astype(F32)

    usend[...] = lax.fori_loop(0, COLUMN, fold_in, jnp.zeros(usend.shape, F32))

    def u_copy(step):
        return remote(usend, urecv.at[column], u_send.at[step], u_recv.at[step], row_peer(step))

    lax.fori_loop(1, COLUMNS, start(u_copy), 0)
    urecv[column] = usend[...]

    @pl.when(z_lo == 0)
    def _():
        relay_far(2)

    slice_rows = pl.ds(pl.multiple_of(rung * (dh // COLUMN), dh // COLUMN), dh // COLUMN)
    state = jnp.concatenate(
        [fin_ref[z_lo, slice_rows].astype(F32), fout_ref[z_lo, slice_rows].astype(F32)], axis=-1
    )
    kept = [
        lax.fori_loop(0, COLUMN, lambda r, f: f * pair_decay(c, r), jnp.float32(1.0))
        for c in range(COLUMNS - 1)
    ]
    lax.fori_loop(1, COLUMNS, wait_got(u_copy), 0)
    for c in range(COLUMNS - 1):
        passed = c < column
        state = jnp.where(passed, kept[c], 1.0) * state + jnp.where(passed, 1.0, 0.0) * urecv[c]

    def advance(r, state):
        ssend[r] = state.astype(BF16)
        return pair_decay(column, r) * state + trecv[r].astype(F32)

    lax.fori_loop(0, COLUMN, advance, state)

    def s_copy(step):
        target = lax.rem(rung + step, COLUMN)
        return remote(
            ssend.at[target], srecv.at[rung], s_send.at[step], s_recv.at[step], column_peer(step)
        )

    lax.fori_loop(1, COLUMN, start(s_copy), 0)
    srecv[rung] = ssend[rung]

    @pl.when(z_lo == 1)
    def _():
        far_copy(2 * pieces - 4).start()
        relay_far(3)
        relay_far(2)

    relay_far(1)
    relay_far(0)

    @pl.when(z_lo == 0)
    def _():
        for i in reversed(range(pieces - 1)):
            far_copy(i).start()

    span = 2 * block_len + ROWS
    first_valid = jnp.where(pair == 0, 2 * block_len, 0)
    scale = LOG2E * dh ** (-0.5)

    def attend(j):
        row0 = pl.multiple_of(j * ROWS, ROWS)
        local_valid = first_valid - row0
        row_ids = lax.broadcasted_iota(jnp.int32, (ROWS, ROWS), 0)
        col_ids = lax.broadcasted_iota(jnp.int32, (ROWS, ROWS), 1)
        middle_ids = lax.broadcasted_iota(jnp.int32, (1, span - 2 * ROWS), 1) + ROWS
        middle_bias = jnp.where(middle_ids >= local_valid, 0.0, -1e30).astype(F32)
        scores = dot_nt(qh[pl.ds(row0, ROWS)], kv[0, pl.ds(row0, span)])
        head_part = jnp.where(
            (col_ids > row_ids) & (col_ids >= local_valid), scores[:, :ROWS], -1e30
        )
        middle_part = scores[:, ROWS : span - ROWS] + middle_bias
        tail_part = jnp.where(col_ids <= row_ids, scores[:, span - ROWS :], -1e30)
        scores = jnp.concatenate([head_part, middle_part, tail_part], axis=-1)
        highest = jnp.max(scores, axis=-1, keepdims=True)
        weights = jnp.exp2((scores - highest) * scale).astype(BF16)
        values = kv[1, pl.ds(row0, span)]
        summed = dot(weights, jnp.concatenate([values, jnp.ones_like(values)], axis=-1))
        return summed[:, :dh] / summed[:, dh:]

    def recall(j, parity):
        queries = qh[pl.ds(pl.multiple_of(j * ROWS, ROWS), ROWS)].astype(F32)
        norm = lax.rsqrt(jnp.sum(queries * queries, axis=-1, keepdims=True) + EPSILON)
        raw = dot((queries * norm).astype(BF16), states[parity, :, : 2 * dh])
        gate = raw[:, :dh]
        hidden = (gate * jax.nn.sigmoid(gate) * raw[:, dh:]).astype(BF16)
        recalled = dot(hidden, states[parity, :, 2 * dh :])
        mean_square = jnp.mean(recalled * recalled, axis=-1, keepdims=True) + EPSILON
        return recalled * lax.rsqrt(mean_square) * gain

    def arrivals(which):
        return (
            head_of(-1, which, z_lo), head_of(1, which, z_lo), head_of(2, which, z_lo),
            head_of(z_lo - 1, which, 1 - z_lo), head_of(z_lo, which, 1 - z_lo),
            head_of(z_lo - 2, which, 1 - z_lo), head_of(z_lo + 1, which, 1 - z_lo),
        )

    own_head = head_of(0, core, z_lo)
    twin_head = head_of(0, 1 - core, z_lo)
    heads_in = arrivals(core)
    twin_heads = (twin_head,) + arrivals(1 - core)

    def piece_of(i):
        return pl.ds(pl.multiple_of(i * ROWS, ROWS), ROWS)

    def g_copy(kind, src, head, i, device_id):
        return remote(src, gath.at[head, piece_of(i)], g_send.at[kind, i], g_recv.at[kind, i], device_id)

    def pass_on(kind, from_kind, i, device_id):
        head = heads_in[from_kind]
        return g_copy(kind, gath.at[head, piece_of(i)], head, i, device_id)

    def got(kind, i):
        head = heads_in[kind] if kind < 7 else twin_heads[kind - 7]
        g_copy(kind, gath.at[head, piece_of(i)], head, i, twin).wait_recv()

    def finish(j, attended, parity):
        i = j - parity * pieces
        row = piece_of(i)
        mixed = (attended + recall(j, parity)).astype(BF16)
        comb[parity, row] = mixed
        src = comb.at[parity, row]

        @pl.when(z_lo == parity)
        def _():
            gath[own_head, row] = mixed
            g_copy(0, src, own_head, i, up2).start()
            g_copy(1, src, own_head, i, down2).start()
            g_copy(7, src, own_head, i, twin).start()

        @pl.when(z_lo != parity)
        def _():
            g_copy(3, src, own_head, i, up1).start()
            g_copy(4, src, own_head, i, down1).start()

    loads[8].wait()
    loads[9].wait()
    gain = jnp.where(lower, gain_ref[:, :dh], gain_ref[:, dh:])
    lax.fori_loop(1, COLUMN, wait_got(s_copy), 0)
    states[0] = srecv[...].reshape(dh, 3 * dh)
    states[1] = (decay_at(2 * pair) * states[0].astype(F32) + dpair[0].astype(F32)).astype(BF16)

    for parity in (1, 0):

        def one(step, _):
            i = pieces - 1 - step
            j = i + parity * pieces

            @pl.when(z_lo != parity)
            def _():
                q_copy(i).wait_recv()

            far_copy(j).wait_recv()
            finish(j, attend(j), parity)
            return 0

        lax.fori_loop(0, pieces, one, 0)

    def relay(step, _):
        for odd in (1, 0):
            i = pieces - 2 - 2 * step + odd
            got(0, i)
            if odd == 0:
                pass_on(2, 0, i, up2).start()
            pass_on(8, 0, i, twin).start()
            got(1, i)
            if odd == 1:
                pass_on(2, 1, i, down2).start()
            pass_on(9, 1, i, twin).start()
            got(3, i)
            pass_on(5, 3, i, up2).start()
            pass_on(11, 3, i, twin).start()
            got(4, i)
            pass_on(6, 4, i, down2).start()
            pass_on(12, 4, i, twin).start()
        return 0

    lax.fori_loop(0, pieces // 2, relay, 0)

    def last_hop(step, _):
        i = pieces - 1 - step
        for kind in (2, 5, 6):
            got(kind, i)
            pass_on(kind + 8, kind, i, twin).start()
        return 0

    lax.fori_loop(0, pieces, last_hop, 0)
    loads[10].wait()

    def project(step, _):
        i = pieces - 1 - step
        for kind in range(7, 15):
            got(kind, i)
        row = piece_of(i)
        total = jnp.zeros((ROWS, o_ref.shape[1]), F32)
        for g in range(0, HEADS, 2):
            both = jnp.concatenate([gath[g, row], gath[g + 1, row]], axis=-1)
            total += dot(both, w_ref[g * dh : (g + 2) * dh, :])
        o_ref[row, :] = total.astype(BF16)
        return 0

    lax.fori_loop(0, pieces, project, 0)

    d_copy.wait_send()

    def drain_gather(i, _):
        for kind in range(15):
            g_copy(kind, comb.at[0, piece_of(i)], own_head, i, twin).wait_send()
        return 0

    lax.fori_loop(0, pieces, wait_sent(e_copy), 0)
    lax.fori_loop(0, pieces, wait_sent(q_copy), 0)
    lax.fori_loop(0, 2 * pieces, wait_sent(far_copy), 0)
    lax.fori_loop(1, COLUMN, wait_sent(t_copy), 0)
    lax.fori_loop(1, COLUMNS, wait_sent(u_copy), 0)
    lax.fori_loop(1, COLUMN, wait_sent(s_copy), 0)
    lax.fori_loop(0, pieces, drain_gather, 0)


def local(queries, keys, values, rates, decays, fast_in, fast_out, ttt_gain, out_weight):
    seq_count, block_len, width = queries.shape
    heads_here, dh, _ = fast_in.shape
    pieces = block_len // ROWS
    state_shape = (dh, 3 * dh)
    slices_shape = (COLUMN, dh // COLUMN, 3 * dh)
    hbm = pl.BlockSpec(memory_space=pltpu.HBM)
    dma = pltpu.SemaphoreType.DMA
    vmem = pltpu.VMEM
    out = pl.pallas_call(
        layer_kernel,
        out_shape=jax.ShapeDtypeStruct((block_len, width), BF16),
        in_specs=[hbm, hbm, hbm, hbm, pl.BlockSpec(memory_space=pltpu.SMEM), hbm, hbm, hbm, hbm],
        out_specs=pl.BlockSpec(memory_space=pltpu.VMEM),
        scratch_shapes=[
            vmem((2, 4 * block_len, dh), BF16),
            vmem((2 * block_len, dh), BF16),
            vmem((3, block_len, dh), BF16),
            vmem((heads_here, block_len), F32),
            vmem((block_len, 8), F32),
            vmem(fast_in.shape, BF16),
            vmem(fast_out.shape, BF16),
            vmem((1, width), F32),
            vmem(out_weight.shape, BF16),
            vmem(state_shape, BF16),
            vmem((2,) + state_shape, BF16),
            vmem(slices_shape, BF16),
            vmem(slices_shape, BF16),
            vmem(slices_shape[1:], F32),
            vmem((COLUMNS,) + slices_shape[1:], F32),
            vmem(slices_shape, BF16),
            vmem(slices_shape, BF16),
            vmem((2,) + state_shape, BF16),
            vmem((2, block_len, dh), BF16),
            vmem((HEADS, block_len, dh), BF16),
            dma((11,)), dma((2,)),
            dma((pieces,)), dma((pieces,)),
            dma((pieces,)), dma((pieces,)), dma((2 * pieces,)), dma((2 * pieces,)),
            dma((COLUMN,)), dma((COLUMN,)), dma((COLUMNS,)), dma((COLUMNS,)),
            dma((COLUMN,)), dma((COLUMN,)),
            dma((15, pieces)), dma((15, pieces)),
        ],
        compiler_params=pltpu.CompilerParams(
            collective_id=0, has_side_effects=True, vmem_limit_bytes=63 << 20
        ),
        name="layer",
    )(
        queries.reshape(block_len, width), keys.reshape(block_len, width), values.reshape(block_len, width),
        rates.reshape(heads_here, block_len), decays.reshape(heads_here, -1),
        fast_in, fast_out, ttt_gain.reshape(1, width), out_weight,
    )
    return out.reshape(seq_count, block_len, width)


def solution(mesh):
    placed = (
        P(None, "seq", "head"),
        P(None, "seq", "head"),
        P(None, "seq", "head"),
        P(None, "head", "seq"),
        P(None, "head", None),
        P("head", None, None),
        P("head", None, None),
        P("head"),
        P(None, "head"),
    )
    return jax.shard_map(
        local, mesh=mesh, in_specs=placed, out_specs=P(None, "seq", "head"), check_vma=False
    )
```

```python
import jax
import jax.numpy as jnp
from jax import lax
from jax.experimental import pallas as pl
from jax.experimental.pallas import tpu as pltpu
from jax.sharding import PartitionSpec as P

EPSILON = 1e-06
MESH = pl.DeviceIdType.MESH
F32 = jnp.float32
BF16 = jnp.bfloat16

COLUMN = 8
COLUMNS = 4
HEADS = 16
ROWS = 256
LOG2E = 1.4426950408889634

EARLY = {4: 3, 0: 2}

UPPER_STOPS = (0, 1, 3, 3, 8)
LOWER_STOPS = (0, 1, 2, 3, 8)


def remote(src, dst, send_sem, recv_sem, device_id):
    return pltpu.make_async_remote_copy(
        src_ref=src,
        dst_ref=dst,
        send_sem=send_sem,
        recv_sem=recv_sem,
        device_id=device_id,
        device_id_type=MESH,
    )


def dot(a, b):
    return jnp.dot(a, b, preferred_element_type=F32)


def dot_nt(a, b):
    return lax.dot_general(a, b, (((1,), (1,)), ((), ())), preferred_element_type=F32)


def dot_tn(a, b):
    return lax.dot_general(a, b, (((0,), (0,)), ((), ())), preferred_element_type=F32)


def layer_kernel(
    q_hbm, k_hbm, v_hbm, rates_hbm, decays_ref, fin_hbm, fout_hbm, gain_hbm, w_hbm, o_hbm,
    kv, qh, spare, rates_ref, rate_cols, fin_ref, fout_ref, gain_ref, w_ref,
    dsend, dpair, tsend, trecv, usend, urecv, ssend, srecv, states, comb, gath, out_ref,
    load_sem, pair_sem, q_send, q_recv, e_send, e_recv, far_send, far_recv, t_send, t_recv,
    u_send, u_recv, s_send, s_recv, g_send, g_recv, out_sem,
):
    place = lax.axis_index("seq")
    head_place = lax.axis_index("head")
    blocks = 2 * COLUMN * COLUMNS
    block_len = q_hbm.shape[0]
    dh = fin_ref.shape[1]
    pieces = block_len // ROWS
    z_lo = lax.rem(place, 2)
    pair = lax.div(place, 2)
    rung = lax.rem(pair, COLUMN)
    column = lax.div(pair, COLUMN)
    z_hi = lax.div(head_place, 2)
    core = lax.rem(head_place, 2)
    partner = place + 1 - 2 * z_lo
    two_on = lax.rem(place + 2, blocks)
    two_back = lax.rem(place + blocks - 2, blocks)

    def at(hops, which):
        return lax.rem(z_hi + hops + 8, 4) * 2 + which

    def head_of(hops, which, low):
        return lax.rem(z_hi + hops + 8, 4) * 4 + which * 2 + low

    up2 = {"head": at(1, core)}
    down2 = {"head": at(-1, core)}
    twin = {"head": at(0, 1 - core)}
    up1 = {"seq": partner, "head": at(z_lo, core)}
    down1 = {"seq": partner, "head": at(z_lo - 1, core)}

    def column_peer(step):
        return {"seq": (column * COLUMN + lax.rem(rung + step, COLUMN)) * 2 + z_lo}

    def row_peer(step):
        return {"seq": (lax.rem(column + step, COLUMNS) * COLUMN + rung) * 2 + z_lo}

    mine = pl.ds(pl.multiple_of(z_lo * dh, dh), dh)
    other = pl.ds(pl.multiple_of((1 - z_lo) * dh, dh), dh)
    own_row = pl.multiple_of(z_lo * block_len, block_len)
    own_base = pl.multiple_of(2 * block_len + z_lo * block_len, block_len)
    own_rows = pl.ds(own_base, block_len)
    load_list = [
        (k_hbm.at[:, mine], kv.at[0, own_rows]),
        (v_hbm.at[:, mine], kv.at[1, own_rows]),
        (k_hbm.at[:, other], spare.at[0]),
        (v_hbm.at[:, other], spare.at[1]),
        (rates_hbm, rates_ref),
        (fin_hbm, fin_ref),
        (fout_hbm, fout_ref),
        (q_hbm.at[:, other], spare.at[2]),
        (q_hbm.at[:, mine], qh.at[pl.ds(own_row, block_len)]),
        (gain_hbm, gain_ref),
        (w_hbm, w_ref),
    ]
    loads = [
        pltpu.make_async_copy(src, dst, load_sem.at[i]) for i, (src, dst) in enumerate(load_list)
    ]
    for load in loads:
        load.start()

    barrier = pltpu.get_barrier_semaphore()

    def greet(device_id):
        pl.semaphore_signal(barrier, inc=1, device_id=device_id, device_id_type=MESH)

    def greet_column(step, _):
        greet(column_peer(step))
        return 0

    def greet_row(step, _):
        greet(row_peer(step))
        return 0

    lax.fori_loop(1, COLUMN, greet_column, 0)
    lax.fori_loop(1, COLUMNS, greet_row, 0)
    for device_id in ({"seq": two_on}, {"seq": two_back}, up1, down1, up2, down2, twin):
        greet(device_id)
    for load in loads[:7]:
        load.wait()

    lower = z_lo == 0
    rates_mine = jnp.where(lower, rates_ref[0:1, :], rates_ref[1:2, :])
    rates_other = jnp.where(lower, rates_ref[1:2, :], rates_ref[0:1, :])
    rate_cols[...] = jnp.transpose(jnp.concatenate([rates_mine, rates_other] * 4, axis=0))
    for which in (1, 0):
        w_in = fin_ref[1 - z_lo] if which else fin_ref[z_lo]
        w_out = fout_ref[1 - z_lo] if which else fout_ref[z_lo]
        d_in = d_out = None
        for r in range(0, block_len, ROWS):
            if which:
                keys, values = spare[0, r : r + ROWS], spare[1, r : r + ROWS]
            else:
                rows = pl.ds(pl.multiple_of(own_base + r, ROWS), ROWS)
                keys, values = kv[0, rows], kv[1, rows]
            keys, values = keys.astype(F32), values.astype(F32)
            norm = lax.rsqrt(jnp.sum(keys * keys, axis=-1, keepdims=True) + EPSILON)
            key_unit = (keys * norm).astype(BF16)
            raw = dot(key_unit, w_in)
            gate, up = raw[:, :dh], raw[:, dh:]
            sig = jax.nn.sigmoid(gate)
            hidden = (gate * sig * up).astype(BF16)
            signal = (rate_cols[r : r + ROWS, which : which + 1] * values).astype(BF16)
            back = dot_nt(signal, w_out)
            grad = jnp.concatenate(
                [
                    (back * up * sig * (1.0 + gate * (1.0 - sig))).astype(BF16),
                    (back * gate * sig).astype(BF16),
                ],
                axis=-1,
            )
            part_in, part_out = dot_tn(key_unit, grad), dot_tn(hidden, signal)
            d_in = part_in if d_in is None else d_in + part_in
            d_out = part_out if d_out is None else d_out + part_out
        delta = jnp.concatenate([d_in, d_out], axis=-1).astype(BF16)
        if which:
            dsend[...] = delta
        else:
            dpair[z_lo] = delta

    pl.semaphore_wait(barrier, (COLUMN - 1) + (COLUMNS - 1) + 7)

    pair_device = {"seq": partner}

    def start(make):
        def one(step, _):
            make(step).start()
            return 0
        return one

    def wait_sent(make):
        def one(step, _):
            make(step).wait_send()
            return 0
        return one

    def wait_got(make):
        def one(step, _):
            make(step).wait_recv()
            return 0
        return one

    d_copy = remote(dsend, dpair.at[z_lo], pair_sem.at[0], pair_sem.at[1], pair_device)

    def q_copy(i):
        row = pl.multiple_of(i * ROWS, ROWS)
        return remote(
            spare.at[2, pl.ds(row, ROWS)],
            qh.at[pl.ds(pl.multiple_of(own_row + row, ROWS), ROWS)],
            q_send.at[i], q_recv.at[i], pair_device,
        )

    def e_copy(i):
        row = pl.multiple_of(i * ROWS, ROWS)
        return remote(
            spare.at[pl.ds(0, 2), pl.ds(row, ROWS)],
            kv.at[:, pl.ds(pl.multiple_of(own_base + row, ROWS), ROWS)],
            e_send.at[i], e_recv.at[i], pair_device,
        )

    def far_copy(c):
        row = pl.multiple_of(c * ROWS, ROWS)
        return remote(
            kv.at[:, pl.ds(pl.multiple_of(2 * block_len + row, ROWS), ROWS)],
            kv.at[:, pl.ds(row, ROWS)],
            far_send.at[c], far_recv.at[c], {"seq": two_on},
        )

    def relay_far(i):
        e_copy(i).wait_recv()
        far_copy((1 - z_lo) * pieces + i).start()

    d_copy.start()

    def own_piece(c):
        return lambda: far_copy(c).start()

    def got_piece(i):
        return lambda: relay_far(i)

    upper_order = [own_piece(2 * pieces - 1 - n) for n in range(pieces)]
    upper_order += [got_piece(pieces - 1 - n) for n in range(pieces)]
    lower_order = [own_piece(pieces - 1)]
    lower_order += [got_piece(pieces - 1 - n) for n in range(pieces)]
    lower_order += [own_piece(pieces - 2 - n) for n in range(pieces - 1)]

    def send_far(stage):
        @pl.when(z_lo == 1)
        def _():
            for send in upper_order[UPPER_STOPS[stage] : UPPER_STOPS[stage + 1]]:
                send()

        @pl.when(z_lo == 0)
        def _():
            for send in lower_order[LOWER_STOPS[stage] : LOWER_STOPS[stage + 1]]:
                send()

    send_far(0)

    loads[7].wait()
    for i in reversed(range(pieces)):
        e_copy(i).start()
    for i in reversed(range(pieces)):
        q_copy(i).start()

    def decay_at(block):
        return decays_ref[z_lo, block]

    def pair_decay(c, r):
        first = (c * COLUMN + r) * 2
        return decay_at(first) * decay_at(first + 1)

    d_copy.wait_recv()
    pair_sum = decay_at(2 * pair + 1) * dpair[0].astype(F32) + dpair[1].astype(F32)
    tsend[...] = pair_sum.astype(BF16).reshape(tsend.shape)

    def t_copy(step):
        target = lax.rem(rung + step, COLUMN)
        return remote(
            tsend.at[target], trecv.at[rung], t_send.at[step], t_recv.at[step], column_peer(step)
        )

    lax.fori_loop(1, COLUMN, start(t_copy), 0)
    trecv[rung] = tsend[rung]

    send_far(1)
    lax.fori_loop(1, COLUMN, wait_got(t_copy), 0)

    def fold_in(r, total):
        return pair_decay(column, r) * total + trecv[r].astype(F32)

    usend[...] = lax.fori_loop(0, COLUMN, fold_in, jnp.zeros(usend.shape, F32))

    def u_copy(step):
        return remote(usend, urecv.at[column], u_send.at[step], u_recv.at[step], row_peer(step))

    lax.fori_loop(1, COLUMNS, start(u_copy), 0)
    urecv[column] = usend[...]
    send_far(2)

    slice_rows = pl.ds(pl.multiple_of(rung * (dh // COLUMN), dh // COLUMN), dh // COLUMN)
    state = jnp.concatenate(
        [fin_ref[z_lo, slice_rows].astype(F32), fout_ref[z_lo, slice_rows].astype(F32)], axis=-1
    )
    kept = [
        lax.fori_loop(0, COLUMN, lambda r, f: f * pair_decay(c, r), jnp.float32(1.0))
        for c in range(COLUMNS - 1)
    ]
    lax.fori_loop(1, COLUMNS, wait_got(u_copy), 0)
    for c in range(COLUMNS - 1):
        passed = c < column
        state = jnp.where(passed, kept[c], 1.0) * state + jnp.where(passed, 1.0, 0.0) * urecv[c]

    def advance(r, state):
        ssend[r] = state.astype(BF16)
        return pair_decay(column, r) * state + trecv[r].astype(F32)

    lax.fori_loop(0, COLUMN, advance, state)

    def s_copy(step):
        target = lax.rem(rung + step, COLUMN)
        return remote(
            ssend.at[target], srecv.at[rung], s_send.at[step], s_recv.at[step], column_peer(step)
        )

    lax.fori_loop(1, COLUMN, start(s_copy), 0)
    srecv[rung] = ssend[rung]

    send_far(3)

    span = 2 * block_len + ROWS
    first_valid = jnp.where(pair == 0, 2 * block_len, 0)
    scale = LOG2E * dh ** (-0.5)

    def attend(j):
        row0 = pl.multiple_of(j * ROWS, ROWS)
        local_valid = first_valid - row0
        row_ids = lax.broadcasted_iota(jnp.int32, (ROWS, ROWS), 0)
        col_ids = lax.broadcasted_iota(jnp.int32, (ROWS, ROWS), 1)
        middle_ids = lax.broadcasted_iota(jnp.int32, (1, span - 2 * ROWS), 1) + ROWS
        middle_bias = jnp.where(middle_ids >= local_valid, 0.0, -1e30).astype(F32)
        scores = dot_nt(qh[pl.ds(row0, ROWS)], kv[0, pl.ds(row0, span)])
        head_part = jnp.where(
            (col_ids > row_ids) & (col_ids >= local_valid), scores[:, :ROWS], -1e30
        )
        middle_part = scores[:, ROWS : span - ROWS] + middle_bias
        tail_part = jnp.where(col_ids <= row_ids, scores[:, span - ROWS :], -1e30)
        scores = jnp.concatenate([head_part, middle_part, tail_part], axis=-1)
        highest = jnp.max(scores, axis=-1, keepdims=True)
        weights = jnp.exp2((scores - highest) * scale).astype(BF16)
        values = kv[1, pl.ds(row0, span)]
        summed = dot(weights, jnp.concatenate([values, jnp.ones_like(values)], axis=-1))
        return summed[:, :dh] / summed[:, dh:]

    def recall(j, parity):
        queries = qh[pl.ds(pl.multiple_of(j * ROWS, ROWS), ROWS)].astype(F32)
        norm = lax.rsqrt(jnp.sum(queries * queries, axis=-1, keepdims=True) + EPSILON)
        raw = dot((queries * norm).astype(BF16), states[parity, :, : 2 * dh])
        gate = raw[:, :dh]
        hidden = (gate * jax.nn.sigmoid(gate) * raw[:, dh:]).astype(BF16)
        recalled = dot(hidden, states[parity, :, 2 * dh :])
        mean_square = jnp.mean(recalled * recalled, axis=-1, keepdims=True) + EPSILON
        return recalled * lax.rsqrt(mean_square) * gain

    def arrivals(which):
        return (
            head_of(-1, which, z_lo), head_of(1, which, z_lo), head_of(2, which, z_lo),
            head_of(z_lo - 1, which, 1 - z_lo), head_of(z_lo, which, 1 - z_lo),
            head_of(z_lo - 2, which, 1 - z_lo), head_of(z_lo + 1, which, 1 - z_lo),
        )

    own_head = head_of(0, core, z_lo)
    twin_head = head_of(0, 1 - core, z_lo)
    heads_in = arrivals(core)
    twin_heads = (twin_head,) + arrivals(1 - core)

    def piece_of(i):
        return pl.ds(pl.multiple_of(i * ROWS, ROWS), ROWS)

    def g_copy(kind, src, head, i, device_id):
        return remote(src, gath.at[head, piece_of(i)], g_send.at[kind, i], g_recv.at[kind, i], device_id)

    def pass_on(kind, from_kind, i, device_id):
        head = heads_in[from_kind]
        return g_copy(kind, gath.at[head, piece_of(i)], head, i, device_id)

    def got(kind, i):
        head = heads_in[kind] if kind < 7 else twin_heads[kind - 7]
        g_copy(kind, gath.at[head, piece_of(i)], head, i, twin).wait_recv()

    def finish(j, attended, parity):
        i = j - parity * pieces
        row = piece_of(i)
        mixed = (attended + recall(j, parity)).astype(BF16)
        comb[parity, row] = mixed
        src = comb.at[parity, row]

        @pl.when(z_lo == parity)
        def _():
            gath[own_head, row] = mixed
            g_copy(0, src, own_head, i, up2).start()
            g_copy(1, src, own_head, i, down2).start()
            g_copy(7, src, own_head, i, twin).start()

        @pl.when(z_lo != parity)
        def _():
            g_copy(3, src, own_head, i, up1).start()
            g_copy(4, src, own_head, i, down1).start()

    loads[8].wait()
    loads[9].wait()
    gain = jnp.where(lower, gain_ref[:, :dh], gain_ref[:, dh:])
    lax.fori_loop(1, COLUMN, wait_got(s_copy), 0)
    states[0] = srecv[...].reshape(dh, 3 * dh)
    states[1] = (decay_at(2 * pair) * states[0].astype(F32) + dpair[0].astype(F32)).astype(BF16)

    def relay(i):
        got(0, i)
        if i % 2 == 0:
            pass_on(2, 0, i, up2).start()
        pass_on(8, 0, i, twin).start()
        got(1, i)
        if i % 2 == 1:
            pass_on(2, 1, i, down2).start()
        pass_on(9, 1, i, twin).start()
        got(3, i)
        pass_on(5, 3, i, up2).start()
        pass_on(11, 3, i, twin).start()
        got(4, i)
        pass_on(6, 4, i, down2).start()
        pass_on(12, 4, i, twin).start()

    waited = 2 * pieces
    for j in (7, 6, 3, 5, 2, 4, 1, 0):
        parity, i = divmod(j, pieces)

        @pl.when(z_lo != parity)
        def _():
            q_copy(i).wait_recv()

        while waited > j:
            waited -= 1
            far_copy(waited).wait_recv()
        finish(j, attend(j), parity)
        if j in EARLY:

            @pl.when(z_lo == 1)
            def _():
                relay(EARLY[j])

    for i in reversed(range(pieces)):
        if i in EARLY.values():

            @pl.when(z_lo == 0)
            def _():
                relay(i)

        else:
            relay(i)

    loads[10].wait()

    def out_copy(i):
        return pltpu.make_async_copy(out_ref.at[piece_of(i)], o_hbm.at[piece_of(i)], out_sem.at[i])

    def project(i):
        for kind in range(7, 15):
            got(kind, i)
        row = piece_of(i)
        total = jnp.zeros((ROWS, out_ref.shape[1]), F32)
        for g in range(0, HEADS, 2):
            both = jnp.concatenate([gath[g, row], gath[g + 1, row]], axis=-1)
            total += dot(both, w_ref[g * dh : (g + 2) * dh, :])
        out_ref[row, :] = total.astype(BF16)
        out_copy(i).start()

    def last_hop(step, _):
        i = pieces - 1 - step
        for kind in (2, 5, 6):
            got(kind, i)
            pass_on(kind + 8, kind, i, twin).start()

        @pl.when(step > 0)
        def _():
            project(i + 1)

        return 0

    lax.fori_loop(0, pieces, last_hop, 0)
    project(0)

    d_copy.wait_send()

    def drain_gather(i, _):
        for kind in range(15):
            g_copy(kind, comb.at[0, piece_of(i)], own_head, i, twin).wait_send()
        return 0

    lax.fori_loop(0, pieces, wait_sent(e_copy), 0)
    lax.fori_loop(0, pieces, wait_sent(q_copy), 0)
    lax.fori_loop(0, 2 * pieces, wait_sent(far_copy), 0)
    lax.fori_loop(1, COLUMN, wait_sent(t_copy), 0)
    lax.fori_loop(1, COLUMNS, wait_sent(u_copy), 0)
    lax.fori_loop(1, COLUMN, wait_sent(s_copy), 0)
    lax.fori_loop(0, pieces, drain_gather, 0)
    for i in range(pieces):
        out_copy(i).wait()


def local(queries, keys, values, rates, decays, fast_in, fast_out, ttt_gain, out_weight):
    seq_count, block_len, width = queries.shape
    heads_here, dh, _ = fast_in.shape
    pieces = block_len // ROWS
    state_shape = (dh, 3 * dh)
    slices_shape = (COLUMN, dh // COLUMN, 3 * dh)
    hbm = pl.BlockSpec(memory_space=pltpu.HBM)
    dma = pltpu.SemaphoreType.DMA
    vmem = pltpu.VMEM
    out = pl.pallas_call(
        layer_kernel,
        out_shape=jax.ShapeDtypeStruct((block_len, width), BF16),
        in_specs=[hbm, hbm, hbm, hbm, pl.BlockSpec(memory_space=pltpu.SMEM), hbm, hbm, hbm, hbm],
        out_specs=hbm,
        scratch_shapes=[
            vmem((2, 4 * block_len, dh), BF16),
            vmem((2 * block_len, dh), BF16),
            vmem((3, block_len, dh), BF16),
            vmem((heads_here, block_len), F32),
            vmem((block_len, 8), F32),
            vmem(fast_in.shape, BF16),
            vmem(fast_out.shape, BF16),
            vmem((1, width), F32),
            vmem(out_weight.shape, BF16),
            vmem(state_shape, BF16),
            vmem((2,) + state_shape, BF16),
            vmem(slices_shape, BF16),
            vmem(slices_shape, BF16),
            vmem(slices_shape[1:], F32),
            vmem((COLUMNS,) + slices_shape[1:], F32),
            vmem(slices_shape, BF16),
            vmem(slices_shape, BF16),
            vmem((2,) + state_shape, BF16),
            vmem((2, block_len, dh), BF16),
            vmem((HEADS, block_len, dh), BF16),
            vmem((block_len, width), BF16),
            dma((11,)), dma((2,)),
            dma((pieces,)), dma((pieces,)),
            dma((pieces,)), dma((pieces,)), dma((2 * pieces,)), dma((2 * pieces,)),
            dma((COLUMN,)), dma((COLUMN,)), dma((COLUMNS,)), dma((COLUMNS,)),
            dma((COLUMN,)), dma((COLUMN,)),
            dma((15, pieces)), dma((15, pieces)), dma((pieces,)),
        ],
        compiler_params=pltpu.CompilerParams(
            collective_id=0, has_side_effects=True, vmem_limit_bytes=63 << 20
        ),
        name="layer",
    )(
        queries.reshape(block_len, width), keys.reshape(block_len, width), values.reshape(block_len, width),
        rates.reshape(heads_here, block_len), decays.reshape(heads_here, -1),
        fast_in, fast_out, ttt_gain.reshape(1, width), out_weight,
    )
    return out.reshape(seq_count, block_len, width)


def solution(mesh):
    placed = (
        P(None, "seq", "head"),
        P(None, "seq", "head"),
        P(None, "seq", "head"),
        P(None, "head", "seq"),
        P(None, "head", None),
        P("head", None, None),
        P("head", None, None),
        P("head"),
        P(None, "head"),
    )
    return jax.shard_map(
        local, mesh=mesh, in_specs=placed, out_specs=P(None, "seq", "head"), check_vma=False
    )
```

```python
import jax
import jax.numpy as jnp
from jax import lax
from jax.experimental import pallas as pl
from jax.experimental.pallas import tpu as pltpu
from jax.sharding import PartitionSpec as P

EPSILON = 1e-06
MESH = pl.DeviceIdType.MESH
F32 = jnp.float32
BF16 = jnp.bfloat16

COLUMN = 8
COLUMNS = 4
HEADS = 16
ROWS = 256
LOG2E = 1.4426950408889634

EARLY = {4: 3, 0: 2}

UPPER_STOPS = (0, 1, 3, 3, 8)
LOWER_STOPS = (0, 1, 2, 3, 8)


def remote(src, dst, send_sem, recv_sem, device_id):
    return pltpu.make_async_remote_copy(
        src_ref=src,
        dst_ref=dst,
        send_sem=send_sem,
        recv_sem=recv_sem,
        device_id=device_id,
        device_id_type=MESH,
    )


def dot(a, b):
    return jnp.dot(a, b, preferred_element_type=F32)


def dot_nt(a, b):
    return lax.dot_general(a, b, (((1,), (1,)), ((), ())), preferred_element_type=F32)


def dot_tn(a, b):
    return lax.dot_general(a, b, (((0,), (0,)), ((), ())), preferred_element_type=F32)


def layer_kernel(
    q_hbm, k_hbm, v_hbm, rates_hbm, decays_ref, fin_hbm, fout_hbm, gain_hbm, w_hbm, out_ref,
    kv, qh, spare, rates_ref, rate_cols, fin_ref, fout_ref, gain_ref, w_ref,
    dsend, dpair, tsend, trecv, usend, urecv, ssend, srecv, states, comb, gath,
    load_sem, pair_sem, q_send, q_recv, e_send, e_recv, far_send, far_recv, t_send, t_recv,
    u_send, u_recv, s_send, s_recv, g_send, g_recv,
):
    place = lax.axis_index("seq")
    head_place = lax.axis_index("head")
    blocks = 2 * COLUMN * COLUMNS
    block_len = q_hbm.shape[0]
    dh = fin_ref.shape[1]
    pieces = block_len // ROWS
    z_lo = lax.rem(place, 2)
    pair = lax.div(place, 2)
    rung = lax.rem(pair, COLUMN)
    column = lax.div(pair, COLUMN)
    z_hi = lax.div(head_place, 2)
    core = lax.rem(head_place, 2)
    partner = place + 1 - 2 * z_lo
    two_on = lax.rem(place + 2, blocks)
    two_back = lax.rem(place + blocks - 2, blocks)

    def at(hops, which):
        return lax.rem(z_hi + hops + 8, 4) * 2 + which

    def head_of(hops, which, low):
        return lax.rem(z_hi + hops + 8, 4) * 4 + which * 2 + low

    up2 = {"head": at(1, core)}
    down2 = {"head": at(-1, core)}
    twin = {"head": at(0, 1 - core)}
    up1 = {"seq": partner, "head": at(z_lo, core)}
    down1 = {"seq": partner, "head": at(z_lo - 1, core)}

    def column_peer(step):
        return {"seq": (column * COLUMN + lax.rem(rung + step, COLUMN)) * 2 + z_lo}

    def row_peer(step):
        return {"seq": (lax.rem(column + step, COLUMNS) * COLUMN + rung) * 2 + z_lo}

    mine = pl.ds(pl.multiple_of(z_lo * dh, dh), dh)
    other = pl.ds(pl.multiple_of((1 - z_lo) * dh, dh), dh)
    own_row = pl.multiple_of(z_lo * block_len, block_len)
    own_base = pl.multiple_of(2 * block_len + z_lo * block_len, block_len)
    own_rows = pl.ds(own_base, block_len)
    load_list = [
        (k_hbm.at[:, mine], kv.at[0, own_rows]),
        (v_hbm.at[:, mine], kv.at[1, own_rows]),
        (k_hbm.at[:, other], spare.at[0]),
        (v_hbm.at[:, other], spare.at[1]),
        (rates_hbm, rates_ref),
        (fin_hbm, fin_ref),
        (fout_hbm, fout_ref),
        (q_hbm.at[:, other], spare.at[2]),
        (q_hbm.at[:, mine], qh.at[pl.ds(own_row, block_len)]),
        (gain_hbm, gain_ref),
        (w_hbm, w_ref),
    ]
    loads = [
        pltpu.make_async_copy(src, dst, load_sem.at[i]) for i, (src, dst) in enumerate(load_list)
    ]
    for load in loads:
        load.start()

    barrier = pltpu.get_barrier_semaphore()

    def greet(device_id):
        pl.semaphore_signal(barrier, inc=1, device_id=device_id, device_id_type=MESH)

    def greet_column(step, _):
        greet(column_peer(step))
        return 0

    def greet_row(step, _):
        greet(row_peer(step))
        return 0

    lax.fori_loop(1, COLUMN, greet_column, 0)
    lax.fori_loop(1, COLUMNS, greet_row, 0)
    for device_id in ({"seq": two_on}, {"seq": two_back}, up1, down1, up2, down2, twin):
        greet(device_id)
    for load in loads[:7]:
        load.wait()

    lower = z_lo == 0
    rates_mine = jnp.where(lower, rates_ref[0:1, :], rates_ref[1:2, :])
    rates_other = jnp.where(lower, rates_ref[1:2, :], rates_ref[0:1, :])
    rate_cols[...] = jnp.transpose(jnp.concatenate([rates_mine, rates_other] * 4, axis=0))
    for which in (1, 0):
        w_in = fin_ref[1 - z_lo] if which else fin_ref[z_lo]
        w_out = fout_ref[1 - z_lo] if which else fout_ref[z_lo]
        d_in = d_out = None
        for r in range(0, block_len, ROWS):
            if which:
                keys, values = spare[0, r : r + ROWS], spare[1, r : r + ROWS]
            else:
                rows = pl.ds(pl.multiple_of(own_base + r, ROWS), ROWS)
                keys, values = kv[0, rows], kv[1, rows]
            keys, values = keys.astype(F32), values.astype(F32)
            norm = lax.rsqrt(jnp.sum(keys * keys, axis=-1, keepdims=True) + EPSILON)
            key_unit = (keys * norm).astype(BF16)
            raw = dot(key_unit, w_in)
            gate, up = raw[:, :dh], raw[:, dh:]
            sig = jax.nn.sigmoid(gate)
            hidden = (gate * sig * up).astype(BF16)
            signal = (rate_cols[r : r + ROWS, which : which + 1] * values).astype(BF16)
            back = dot_nt(signal, w_out)
            grad = jnp.concatenate(
                [
                    (back * up * sig * (1.0 + gate * (1.0 - sig))).astype(BF16),
                    (back * gate * sig).astype(BF16),
                ],
                axis=-1,
            )
            part_in, part_out = dot_tn(key_unit, grad), dot_tn(hidden, signal)
            d_in = part_in if d_in is None else d_in + part_in
            d_out = part_out if d_out is None else d_out + part_out
        delta = jnp.concatenate([d_in, d_out], axis=-1).astype(BF16)
        if which:
            dsend[...] = delta
        else:
            dpair[z_lo] = delta

    pl.semaphore_wait(barrier, (COLUMN - 1) + (COLUMNS - 1) + 7)

    pair_device = {"seq": partner}

    def start(make):
        def one(step, _):
            make(step).start()
            return 0
        return one

    def wait_sent(make):
        def one(step, _):
            make(step).wait_send()
            return 0
        return one

    def wait_got(make):
        def one(step, _):
            make(step).wait_recv()
            return 0
        return one

    d_copy = remote(dsend, dpair.at[z_lo], pair_sem.at[0], pair_sem.at[1], pair_device)

    def q_copy(i):
        row = pl.multiple_of(i * ROWS, ROWS)
        return remote(
            spare.at[2, pl.ds(row, ROWS)],
            qh.at[pl.ds(pl.multiple_of(own_row + row, ROWS), ROWS)],
            q_send.at[i], q_recv.at[i], pair_device,
        )

    def e_copy(i):
        row = pl.multiple_of(i * ROWS, ROWS)
        return remote(
            spare.at[pl.ds(0, 2), pl.ds(row, ROWS)],
            kv.at[:, pl.ds(pl.multiple_of(own_base + row, ROWS), ROWS)],
            e_send.at[i], e_recv.at[i], pair_device,
        )

    def far_copy(c):
        row = pl.multiple_of(c * ROWS, ROWS)
        return remote(
            kv.at[:, pl.ds(pl.multiple_of(2 * block_len + row, ROWS), ROWS)],
            kv.at[:, pl.ds(row, ROWS)],
            far_send.at[c], far_recv.at[c], {"seq": two_on},
        )

    def relay_far(i):
        e_copy(i).wait_recv()
        far_copy((1 - z_lo) * pieces + i).start()

    d_copy.start()

    def own_piece(c):
        return lambda: far_copy(c).start()

    def got_piece(i):
        return lambda: relay_far(i)

    upper_order = [own_piece(2 * pieces - 1 - n) for n in range(pieces)]
    upper_order += [got_piece(pieces - 1 - n) for n in range(pieces)]
    lower_order = [own_piece(pieces - 1)]
    lower_order += [got_piece(pieces - 1 - n) for n in range(pieces)]
    lower_order += [own_piece(pieces - 2 - n) for n in range(pieces - 1)]

    def send_far(stage):
        @pl.when(z_lo == 1)
        def _():
            for send in upper_order[UPPER_STOPS[stage] : UPPER_STOPS[stage + 1]]:
                send()

        @pl.when(z_lo == 0)
        def _():
            for send in lower_order[LOWER_STOPS[stage] : LOWER_STOPS[stage + 1]]:
                send()

    send_far(0)

    loads[7].wait()
    for i in reversed(range(pieces)):
        e_copy(i).start()
    for i in reversed(range(pieces)):
        q_copy(i).start()

    def decay_at(block):
        return decays_ref[z_lo, block]

    def pair_decay(c, r):
        first = (c * COLUMN + r) * 2
        return decay_at(first) * decay_at(first + 1)

    d_copy.wait_recv()
    pair_sum = decay_at(2 * pair + 1) * dpair[0].astype(F32) + dpair[1].astype(F32)
    tsend[...] = pair_sum.astype(BF16).reshape(tsend.shape)

    def t_copy(step):
        target = lax.rem(rung + step, COLUMN)
        return remote(
            tsend.at[target], trecv.at[rung], t_send.at[step], t_recv.at[step], column_peer(step)
        )

    lax.fori_loop(1, COLUMN, start(t_copy), 0)
    trecv[rung] = tsend[rung]

    send_far(1)
    lax.fori_loop(1, COLUMN, wait_got(t_copy), 0)

    def fold_in(r, total):
        return pair_decay(column, r) * total + trecv[r].astype(F32)

    usend[...] = lax.fori_loop(0, COLUMN, fold_in, jnp.zeros(usend.shape, F32))

    def u_copy(step):
        return remote(usend, urecv.at[column], u_send.at[step], u_recv.at[step], row_peer(step))

    lax.fori_loop(1, COLUMNS, start(u_copy), 0)
    urecv[column] = usend[...]
    send_far(2)

    slice_rows = pl.ds(pl.multiple_of(rung * (dh // COLUMN), dh // COLUMN), dh // COLUMN)
    state = jnp.concatenate(
        [fin_ref[z_lo, slice_rows].astype(F32), fout_ref[z_lo, slice_rows].astype(F32)], axis=-1
    )
    kept = [
        lax.fori_loop(0, COLUMN, lambda r, f: f * pair_decay(c, r), jnp.float32(1.0))
        for c in range(COLUMNS - 1)
    ]
    lax.fori_loop(1, COLUMNS, wait_got(u_copy), 0)
    for c in range(COLUMNS - 1):
        passed = c < column
        state = jnp.where(passed, kept[c], 1.0) * state + jnp.where(passed, 1.0, 0.0) * urecv[c]

    def advance(r, state):
        ssend[r] = state.astype(BF16)
        return pair_decay(column, r) * state + trecv[r].astype(F32)

    lax.fori_loop(0, COLUMN, advance, state)

    def s_copy(step):
        target = lax.rem(rung + step, COLUMN)
        return remote(
            ssend.at[target], srecv.at[rung], s_send.at[step], s_recv.at[step], column_peer(step)
        )

    lax.fori_loop(1, COLUMN, start(s_copy), 0)
    srecv[rung] = ssend[rung]

    send_far(3)

    span = 2 * block_len + ROWS
    first_valid = jnp.where(pair == 0, 2 * block_len, 0)
    scale = LOG2E * dh ** (-0.5)

    def attend(j):
        row0 = pl.multiple_of(j * ROWS, ROWS)
        local_valid = first_valid - row0
        row_ids = lax.broadcasted_iota(jnp.int32, (ROWS, ROWS), 0)
        col_ids = lax.broadcasted_iota(jnp.int32, (ROWS, ROWS), 1)
        middle_ids = lax.broadcasted_iota(jnp.int32, (1, span - 2 * ROWS), 1) + ROWS
        middle_bias = jnp.where(middle_ids >= local_valid, 0.0, -1e30).astype(F32)
        scores = dot_nt(qh[pl.ds(row0, ROWS)], kv[0, pl.ds(row0, span)])
        head_part = jnp.where(
            (col_ids > row_ids) & (col_ids >= local_valid), scores[:, :ROWS], -1e30
        )
        middle_part = scores[:, ROWS : span - ROWS] + middle_bias
        tail_part = jnp.where(col_ids <= row_ids, scores[:, span - ROWS :], -1e30)
        scores = jnp.concatenate([head_part, middle_part, tail_part], axis=-1)
        highest = jnp.max(scores, axis=-1, keepdims=True)
        weights = jnp.exp2((scores - highest) * scale).astype(BF16)
        values = kv[1, pl.ds(row0, span)]
        summed = dot(weights, jnp.concatenate([values, jnp.ones_like(values)], axis=-1))
        return summed[:, :dh] / summed[:, dh:]

    def recall(j, parity):
        queries = qh[pl.ds(pl.multiple_of(j * ROWS, ROWS), ROWS)].astype(F32)
        norm = lax.rsqrt(jnp.sum(queries * queries, axis=-1, keepdims=True) + EPSILON)
        raw = dot((queries * norm).astype(BF16), states[parity, :, : 2 * dh])
        gate = raw[:, :dh]
        hidden = (gate * jax.nn.sigmoid(gate) * raw[:, dh:]).astype(BF16)
        recalled = dot(hidden, states[parity, :, 2 * dh :])
        mean_square = jnp.mean(recalled * recalled, axis=-1, keepdims=True) + EPSILON
        return recalled * lax.rsqrt(mean_square) * gain

    def arrivals(which):
        return (
            head_of(-1, which, z_lo), head_of(1, which, z_lo), head_of(2, which, z_lo),
            head_of(z_lo - 1, which, 1 - z_lo), head_of(z_lo, which, 1 - z_lo),
            head_of(z_lo - 2, which, 1 - z_lo), head_of(z_lo + 1, which, 1 - z_lo),
        )

    own_head = head_of(0, core, z_lo)
    twin_head = head_of(0, 1 - core, z_lo)
    heads_in = arrivals(core)
    twin_heads = (twin_head,) + arrivals(1 - core)

    def piece_of(i):
        return pl.ds(pl.multiple_of(i * ROWS, ROWS), ROWS)

    def g_copy(kind, src, head, i, device_id):
        return remote(src, gath.at[head, piece_of(i)], g_send.at[kind, i], g_recv.at[kind, i], device_id)

    def pass_on(kind, from_kind, i, device_id):
        head = heads_in[from_kind]
        return g_copy(kind, gath.at[head, piece_of(i)], head, i, device_id)

    def got(kind, i):
        head = heads_in[kind] if kind < 7 else twin_heads[kind - 7]
        g_copy(kind, gath.at[head, piece_of(i)], head, i, twin).wait_recv()

    def finish(j, attended, parity):
        i = j - parity * pieces
        row = piece_of(i)
        mixed = (attended + recall(j, parity)).astype(BF16)
        comb[parity, row] = mixed
        src = comb.at[parity, row]

        @pl.when(z_lo == parity)
        def _():
            gath[own_head, row] = mixed
            g_copy(0, src, own_head, i, up2).start()
            g_copy(1, src, own_head, i, down2).start()
            g_copy(7, src, own_head, i, twin).start()

        @pl.when(z_lo != parity)
        def _():
            g_copy(3, src, own_head, i, up1).start()
            g_copy(4, src, own_head, i, down1).start()

    loads[8].wait()
    loads[9].wait()
    gain = jnp.where(lower, gain_ref[:, :dh], gain_ref[:, dh:])
    lax.fori_loop(1, COLUMN, wait_got(s_copy), 0)
    states[0] = srecv[...].reshape(dh, 3 * dh)
    states[1] = (decay_at(2 * pair) * states[0].astype(F32) + dpair[0].astype(F32)).astype(BF16)

    def relay(i):
        got(0, i)
        if i % 2 == 0:
            pass_on(2, 0, i, up2).start()
        pass_on(8, 0, i, twin).start()
        got(1, i)
        if i % 2 == 1:
            pass_on(2, 1, i, down2).start()
        pass_on(9, 1, i, twin).start()
        got(3, i)
        pass_on(5, 3, i, up2).start()
        pass_on(11, 3, i, twin).start()
        got(4, i)
        pass_on(6, 4, i, down2).start()
        pass_on(12, 4, i, twin).start()

    waited = 2 * pieces
    for j in (7, 6, 5, 3, 4, 2, 1, 0):
        parity, i = divmod(j, pieces)

        @pl.when(z_lo != parity)
        def _():
            q_copy(i).wait_recv()

        while waited > j:
            waited -= 1
            far_copy(waited).wait_recv()
        finish(j, attend(j), parity)
        if j in EARLY:

            @pl.when(z_lo == 1)
            def _():
                relay(EARLY[j])

    for i in reversed(range(pieces)):
        if i in EARLY.values():

            @pl.when(z_lo == 0)
            def _():
                relay(i)

        else:
            relay(i)

    loads[10].wait()

    def project(i):
        for kind in range(7, 15):
            got(kind, i)
        row = piece_of(i)
        total = jnp.zeros((ROWS, out_ref.shape[1]), F32)
        for g in range(0, HEADS, 2):
            both = jnp.concatenate([gath[g, row], gath[g + 1, row]], axis=-1)
            total += dot(both, w_ref[g * dh : (g + 2) * dh, :])
        out_ref[row, :] = total.astype(BF16)

    def last_hop(step, _):
        i = pieces - 1 - step
        for kind in (2, 5, 6):
            got(kind, i)
            pass_on(kind + 8, kind, i, twin).start()

        @pl.when(step > 0)
        def _():
            project(i + 1)

        return 0

    lax.fori_loop(0, pieces, last_hop, 0)
    project(0)

    d_copy.wait_send()

    def drain_gather(i, _):
        for kind in range(15):
            g_copy(kind, comb.at[0, piece_of(i)], own_head, i, twin).wait_send()
        return 0

    lax.fori_loop(0, pieces, wait_sent(e_copy), 0)
    lax.fori_loop(0, pieces, wait_sent(q_copy), 0)
    lax.fori_loop(0, 2 * pieces, wait_sent(far_copy), 0)
    lax.fori_loop(1, COLUMN, wait_sent(t_copy), 0)
    lax.fori_loop(1, COLUMNS, wait_sent(u_copy), 0)
    lax.fori_loop(1, COLUMN, wait_sent(s_copy), 0)
    lax.fori_loop(0, pieces, drain_gather, 0)


def local(queries, keys, values, rates, decays, fast_in, fast_out, ttt_gain, out_weight):
    seq_count, block_len, width = queries.shape
    heads_here, dh, _ = fast_in.shape
    pieces = block_len // ROWS
    state_shape = (dh, 3 * dh)
    slices_shape = (COLUMN, dh // COLUMN, 3 * dh)
    hbm = pl.BlockSpec(memory_space=pltpu.HBM)
    dma = pltpu.SemaphoreType.DMA
    vmem = pltpu.VMEM
    out = pl.pallas_call(
        layer_kernel,
        out_shape=vmem((block_len, width), BF16),
        in_specs=[hbm, hbm, hbm, hbm, pl.BlockSpec(memory_space=pltpu.SMEM), hbm, hbm, hbm, hbm],
        out_specs=pl.BlockSpec(memory_space=pltpu.VMEM),
        scratch_shapes=[
            vmem((2, 4 * block_len, dh), BF16),
            vmem((2 * block_len, dh), BF16),
            vmem((3, block_len, dh), BF16),
            vmem((heads_here, block_len), F32),
            vmem((block_len, 8), F32),
            vmem(fast_in.shape, BF16),
            vmem(fast_out.shape, BF16),
            vmem((1, width), F32),
            vmem(out_weight.shape, BF16),
            vmem(state_shape, BF16),
            vmem((2,) + state_shape, BF16),
            vmem(slices_shape, BF16),
            vmem(slices_shape, BF16),
            vmem(slices_shape[1:], F32),
            vmem((COLUMNS,) + slices_shape[1:], F32),
            vmem(slices_shape, BF16),
            vmem(slices_shape, BF16),
            vmem((2,) + state_shape, BF16),
            vmem((2, block_len, dh), BF16),
            vmem((HEADS, block_len, dh), BF16),
            dma((11,)), dma((2,)),
            dma((pieces,)), dma((pieces,)),
            dma((pieces,)), dma((pieces,)), dma((2 * pieces,)), dma((2 * pieces,)),
            dma((COLUMN,)), dma((COLUMN,)), dma((COLUMNS,)), dma((COLUMNS,)),
            dma((COLUMN,)), dma((COLUMN,)),
            dma((15, pieces)), dma((15, pieces)),
        ],
        compiler_params=pltpu.CompilerParams(
            collective_id=0, has_side_effects=True, vmem_limit_bytes=63 << 20
        ),
        name="layer",
    )(
        queries.reshape(block_len, width), keys.reshape(block_len, width), values.reshape(block_len, width),
        rates.reshape(heads_here, block_len), decays.reshape(heads_here, -1),
        fast_in, fast_out, ttt_gain.reshape(1, width), out_weight,
    )
    return out.reshape(seq_count, block_len, width)


def solution(mesh):
    placed = (
        P(None, "seq", "head"),
        P(None, "seq", "head"),
        P(None, "seq", "head"),
        P(None, "head", "seq"),
        P(None, "head", None),
        P("head", None, None),
        P("head", None, None),
        P("head"),
        P(None, "head"),
    )
    return jax.shard_map(
        local, mesh=mesh, in_specs=placed, out_specs=P(None, "seq", "head"), check_vma=False
    )
```
